512 devices in a mesh: blk: 16 (over x, y_hi, core), wide: 32 (over y_lo, z).
Axes of the slice: x: 4, y: 8 (y_hi: 2, y_lo: 4; y = y_hi * 4 + y_lo), z: 8, core: 2. Of those that a mesh axis runs over, the one named last changes fastest.
Arguments:
- observed: bfloat16 [131072, 5120], P(('blk', 'wide')), may hold values from -8 to 8
- mask_bits: int32 [131072, 640], P(('blk', 'wide')), may hold values from 0 to 255, as said below
- frame_factors: float32 [131072, 256], P(('blk', 'wide')), may hold values from -2 to 2
- pixel_factors: bfloat16 [524288, 256], P(('blk', 'wide')), may hold values from -2 to 2
Outputs:
- frames_out: float32 [131072, 256], P(('blk', 'wide'))
- pixels_out: bfloat16 [524288, 256], P(('blk', 'wide'))
The draws below stay inside these ranges and needn't reach their ends.
Inputs may be any that keep to these rules, and one draw needn't show every extreme that they name: `mask_bits`: each word holds 8 independent flags, each set with probability one half.
All inputs are finite; a program needn't handle non-finite values.
Results may differ from the reference program's by a relative error of at most 0.0071.
Values may be sent and summed in bfloat16 or wider, within the bound.
A program may use at most 64 MiB of HBM per device.

```python
from functools import partial
import jax
import jax.numpy as jnp
from jax import lax

RANK = 256
PB = 1024
VISITS = 5
FR_DEV = 256
FRAMES = 131072
PIXELS = 524288
WORDS = 640
N_BLK = 16
N_WIDE = 32


def draw_mask_bits(key, part):
    values = jax.random.randint(key, (FRAMES, WORDS), 0, 256, dtype=jnp.int32)
    values = values.at[0, 0].set(255)
    return values.at[0, 1].set(0)


def shard_levels(stream_key, extent, shards, smallest, high):
    def one(position, shards_of):
        draws = jax.random.uniform(jax.random.fold_in(jax.random.fold_in(stream_key, 6), position), (shards_of,), jnp.float32, smallest / len(shards), high / len(shards))
        return jnp.repeat(jnp.exp(draws), extent[position] // shards_of).reshape((-1,) + (1,) * (len(extent) - position - 1))

    loudness = one(*shards[0])
    for cut in shards[1:]:
        loudness = loudness * one(*cut)
    return loudness


def scatter_about(own_key, shape, width, reach, split=(), held_as=jnp.bfloat16):
    drawn = width * jax.random.normal(own_key, shape, jnp.float32)
    if split:
        drawn = drawn * shard_levels(own_key, shape, split, -0.22, 0.18)
    return jnp.clip(drawn, -reach, reach).astype(held_as)


def setup_inputs(seed: int = 0) -> dict:
    streams_of = jax.random.split(jax.random.key(seed), 5)
    return {
        "observed": scatter_about(streams_of[0], (FRAMES, VISITS * PB), 1.5, 8.0, ((0, 512),)),
        "mask_bits": draw_mask_bits(jax.random.fold_in(streams_of[4], 71), 0),
        "frame_factors": scatter_about(streams_of[2], (FRAMES, RANK), 0.25, 2.0, ((0, 512),), jnp.float32),
        "pixel_factors": scatter_about(streams_of[3], (PIXELS, RANK), 0.25, 2.0, ((0, 512),)),
    }


clip_level = 1.0
step_frames = 0.01
step_pixels = 0.02
decay_weight = 0.1


def unpack_mask(packed):
    shifts = jnp.arange(8, dtype=jnp.int32)
    expanded = jnp.bitwise_and(jnp.right_shift(packed[..., None, :], shifts[:, None]), 1)
    return expanded.reshape(packed.shape[:-1] + (8 * packed.shape[-1],)).astype(jnp.float32)


def tile_update(visit_index, operands):
    observed_row, packed_row, frames_row, pixels_row = operands
    lower = visit_index * PB
    wanted = observed_row[..., lower:lower + PB].astype(jnp.float32)
    visible = unpack_mask(packed_row)[..., lower:lower + PB]
    frames_low = lax.optimization_barrier(frames_row.astype(jnp.bfloat16)).astype(jnp.float32)
    pixels_wide = pixels_row.astype(jnp.float32)
    predicted = jnp.einsum('wfr,wpr->wfp', frames_low, pixels_wide)
    errors = visible * (wanted - predicted)
    weights = clip_level / jnp.maximum(jnp.abs(errors), clip_level)
    scaled = lax.optimization_barrier((weights * errors).astype(jnp.bfloat16)).astype(jnp.float32)
    grad_frames = jnp.einsum('wfp,wpr->wfr', scaled, pixels_wide)
    grad_pixels = jnp.einsum('wfp,wfr->wpr', scaled, frames_low)
    new_frames = frames_row + step_frames * (grad_frames - decay_weight * frames_row)
    new_pixels = (pixels_wide + step_pixels * (grad_pixels - decay_weight * pixels_wide)).astype(jnp.bfloat16)
    return new_frames, new_pixels


def reference(observed, mask_bits, frame_factors, pixel_factors):
    grid_obs = observed.reshape(N_BLK, N_WIDE, FR_DEV, VISITS * PB)
    grid_bits = mask_bits.reshape(N_BLK, N_WIDE, FR_DEV, WORDS)
    frames = frame_factors.reshape(N_BLK, N_WIDE, FR_DEV, RANK)
    pixels = pixel_factors.reshape(N_BLK, N_WIDE, PB, RANK)
    for visit_index in range(VISITS):
        frames, pixels = lax.map(partial(tile_update, visit_index), (grid_obs, grid_bits, frames, pixels))
        if visit_index < VISITS - 2:
            pixels = jnp.roll(pixels, 1, axis=0)
        elif visit_index == VISITS - 2:
            pixels = jnp.roll(pixels, 1, axis=1)
    return frames.reshape(FRAMES, RANK), pixels.reshape(PIXELS, RANK)
```

```python
import functools

import jax
import jax.numpy as jnp
from jax import lax
from jax.experimental import pallas as pl
from jax.experimental.pallas import tpu as pltpu
from jax.sharding import PartitionSpec as P

VISITS = 5
LANES = 128
CHUNK = 128
MESH = pl.DeviceIdType.MESH

step_frames = 0.01
step_pixels = 0.02
decay_weight = 0.1


def kernel(
    n_blk, n_wide, obs_hbm, bits_hbm, frames_hbm, pixels_hbm, frames_out, pixels_out,
    obs, bits, frames, low, total, held, fresh, load_sem, send_sem, recv_sem,
):
    width = pixels_out.shape[0]
    chunks = width // CHUNK
    groups = bits.shape[1] // LANES
    i, j = lax.axis_index("blk"), lax.axis_index("wide")
    next_blk = (lax.rem(i + 1, n_blk), j)
    last_blk = (lax.rem(i + n_blk - 1, n_blk), j)
    next_wide = (i, lax.rem(j + 1, n_wide))
    last_wide = (i, lax.rem(j + n_wide - 1, n_wide))

    barrier = pltpu.get_barrier_semaphore()
    for peer in (next_blk, last_blk, next_wide, last_wide):
        pl.semaphore_signal(barrier, inc=1, device_id=peer, device_id_type=MESH)

    def load(source, target, index):
        return pltpu.make_async_copy(source, target, load_sem.at[index])

    def load_obs(visit):
        columns = pl.ds(visit * width, width)
        return load(obs_hbm.at[:, columns], obs.at[:, columns], 3 + visit)

    first = [load(frames_hbm, frames, 0), load(pixels_hbm, held.at[0], 1), load(bits_hbm, bits, 2)]
    for copy in first:
        copy.start()
    for visit in range(VISITS):
        load_obs(visit).start()
    for copy in first:
        copy.wait()

    def send(visit, chunk):
        rows = pl.ds(pl.multiple_of(chunk * CHUNK, CHUNK), CHUNK)
        return pltpu.make_async_remote_copy(
            src_ref=fresh.at[visit, rows],
            dst_ref=held.at[visit + 1, rows],
            send_sem=send_sem.at[visit, chunk],
            recv_sem=recv_sem.at[visit, chunk],
            device_id=next_blk if visit < VISITS - 2 else next_wide,
            device_id_type=MESH,
        )

    def update(visit, chunk):
        rows = pl.ds(pl.multiple_of(chunk * CHUNK, CHUNK), CHUNK)
        old = held[visit, rows, :]
        low_frames = low[...]
        predicted = lax.dot_general(
            low_frames, old, (((1,), (1,)), ((), ())), preferred_element_type=jnp.float32
        )
        place = visit * (width // LANES) + chunk
        columns = pl.ds(pl.multiple_of(place * LANES, LANES), LANES)
        words = bits[:, pl.ds(pl.multiple_of(lax.rem(place, groups) * LANES, LANES), LANES)]
        flag = jnp.left_shift(jnp.int32(1), lax.div(place, groups))
        errors = jnp.where((words & flag) != 0, obs[:, columns].astype(jnp.float32) - predicted, 0.0)
        scaled = jnp.clip(errors, -1.0, 1.0).astype(jnp.bfloat16)
        total[...] += jnp.dot(scaled, old, preferred_element_type=jnp.float32)
        grad = lax.dot_general(
            scaled, low_frames, (((0,), (0,)), ((), ())), preferred_element_type=jnp.float32
        )
        wide_old = old.astype(jnp.float32)
        new = (wide_old + step_pixels * (grad - decay_weight * wide_old)).astype(jnp.bfloat16)
        if visit < VISITS - 1:
            fresh[visit, rows, :] = new
        else:
            pixels_out[rows, :] = new

    for visit in range(VISITS):
        low[...] = frames[...].astype(jnp.bfloat16)
        total[...] = jnp.zeros_like(total)
        load_obs(visit).wait()

        if visit == 0:
            @pl.loop(0, chunks)
            def _(chunk):
                update(0, chunk)

            pl.semaphore_wait(barrier, 4)

            @pl.loop(0, chunks)
            def _(chunk):
                send(0, chunk).start()
        else:
            @pl.loop(0, chunks)
            def _(chunk, visit=visit):
                send(visit - 1, chunk).wait_recv()
                update(visit, chunk)
                if visit < VISITS - 1:
                    send(visit, chunk).start()

        current = frames[...]
        updated = current + step_frames * (total[...] - decay_weight * current)
        if visit < VISITS - 1:
            frames[...] = updated
        else:
            frames_out[...] = updated

    for visit in range(VISITS - 1):
        @pl.loop(0, chunks)
        def _(chunk, visit=visit):
            send(visit, chunk).wait_send()


def solution(mesh):
    n_blk, n_wide = mesh.shape["blk"], mesh.shape["wide"]

    def body(observed, mask_bits, frame_factors, pixel_factors):
        width, rank = pixel_factors.shape
        chunks = width // CHUNK
        return tuple(pl.pallas_call(
            functools.partial(kernel, n_blk, n_wide),
            out_shape=(
                jax.ShapeDtypeStruct(frame_factors.shape, frame_factors.dtype),
                jax.ShapeDtypeStruct(pixel_factors.shape, pixel_factors.dtype),
            ),
            in_specs=[pl.BlockSpec(memory_space=pl.ANY)] * 4,
            out_specs=(pl.BlockSpec(memory_space=pltpu.VMEM),) * 2,
            scratch_shapes=[
                pltpu.VMEM(observed.shape, observed.dtype),
                pltpu.VMEM(mask_bits.shape, mask_bits.dtype),
                pltpu.VMEM(frame_factors.shape, jnp.float32),
                pltpu.VMEM(frame_factors.shape, jnp.bfloat16),
                pltpu.VMEM(frame_factors.shape, jnp.float32),
                pltpu.VMEM((VISITS, width, rank), jnp.bfloat16),
                pltpu.VMEM((VISITS - 1, width, rank), jnp.bfloat16),
                pltpu.SemaphoreType.DMA((3 + VISITS,)),
                pltpu.SemaphoreType.DMA((VISITS - 1, chunks)),
                pltpu.SemaphoreType.DMA((VISITS - 1, chunks)),
            ],
            compiler_params=pltpu.CompilerParams(
                collective_id=0, has_side_effects=True
            ),
        )(observed, mask_bits, frame_factors, pixel_factors))

    spec = P(("blk", "wide"), None)
    return jax.shard_map(
        body, mesh=mesh, in_specs=(spec,) * 4, out_specs=(spec, spec), check_vma=False
    )
```

```python
import functools

import jax
import jax.numpy as jnp
from jax import lax
from jax.experimental import pallas as pl
from jax.experimental.pallas import tpu as pltpu
from jax.sharding import PartitionSpec as P

VISITS = 5
LANES = 128
CHUNK = 128
RUN = 8
RELAYED = 8
AHEAD = 5
GBASE = 5
GUESTS = 3
MESH = pl.DeviceIdType.MESH

step_frames = 0.01
step_pixels = 0.02
decay_weight = 0.1


def kernel(
    n_blk, n_wide, obs_hbm, bits_hbm, frames_hbm, pixels_hbm, frames_out, pixels_out,
    obs, bits, frames, low, total, held, fresh, relay, load_sem, send_sem, recv_sem, relay_send, relay_recv,
    guest, guest_send, guest_recv,
):
    width = pixels_out.shape[0]
    chunks = width // CHUNK
    groups = bits.shape[1] // LANES
    i, j = lax.axis_index("blk"), lax.axis_index("wide")
    next_blk = (lax.rem(i + 1, n_blk), j)
    last_blk = (lax.rem(i + n_blk - 1, n_blk), j)
    place = lax.rem(j, RUN)
    is_first, is_last = place == 0, place == RUN - 1
    next_wide = (i, jnp.where(is_last, j - (RUN - 1), j + 1))
    last_wide = (i, jnp.where(is_first, j + (RUN - 1), j - 1))
    next_run = (i, lax.rem(j + RUN, n_wide))
    last_run = (i, lax.rem(j + n_wide - RUN, n_wide))
    right = (i, lax.rem(j + 1, n_wide))
    left = (i, lax.rem(j + n_wide - 1, n_wide))

    barrier = pltpu.get_barrier_semaphore()

    def greet(peer):
        pl.semaphore_signal(barrier, inc=1, device_id=peer, device_id_type=MESH)

    greet(last_blk)

    @pl.when(jnp.logical_not(is_first))
    def _():
        greet(left)

    odd = lax.rem(i, 2) == 1
    even = jnp.logical_not(odd)
    is_host = even & (place < RUN - 1) & (place >= RUN - 1 - GUESTS)
    guest_slot = jnp.where(is_host, RUN - 2 - place, 0)
    guest_from = (lax.rem(i + 1, n_blk), jnp.where(is_host, j + guest_slot + 1, j))
    guest_to = (lax.rem(i + 2, n_blk), guest_from[1])

    def host_of(chunk):
        return (lax.rem(i + n_blk - 1, n_blk), jnp.where(is_last, j - 1 - chunk, j))

    @pl.when(is_host)
    def _():
        greet(guest_from)

    @pl.when(is_last & even)
    def _():
        for chunk in range(GUESTS):
            greet((lax.rem(i + n_blk - 2, n_blk), host_of(chunk)[1]))

    @pl.when(is_first)
    def _():
        greet(last_wide)
        greet(last_run)

    def meet():
        extra = jnp.where(is_host | is_first, 1, jnp.where(is_last & odd, GUESTS, 0))
        pl.semaphore_wait(barrier, 2 + extra)

    def load(source, target, index):
        return pltpu.make_async_copy(source, target, load_sem.at[index])

    def load_obs(visit):
        columns = pl.ds(visit * width, width)
        return load(obs_hbm.at[:, columns], obs.at[:, columns], 3 + visit)

    first = [load(frames_hbm, frames, 0), load(pixels_hbm, held.at[0], 1), load(bits_hbm, bits, 2)]
    for copy in first:
        copy.start()
    for visit in range(VISITS):
        load_obs(visit).start()
    for copy in first:
        copy.wait()

    def send(visit, chunk):
        rows = pl.ds(pl.multiple_of(chunk * CHUNK, CHUNK), CHUNK)
        return pltpu.make_async_remote_copy(
            src_ref=fresh.at[visit, rows],
            dst_ref=held.at[visit + 1, rows],
            send_sem=send_sem.at[visit, chunk],
            recv_sem=recv_sem.at[visit, chunk],
            device_id=next_blk if visit < VISITS - 2 else right,
            device_id_type=MESH,
        )

    def send_around(chunk):
        chunk = jnp.minimum(chunk, RELAYED - 1)
        rows = pl.ds(pl.multiple_of(chunk * CHUNK, CHUNK), CHUNK)
        return pltpu.make_async_remote_copy(
            src_ref=fresh.at[VISITS - 2, rows],
            dst_ref=relay.at[rows],
            send_sem=send_sem.at[VISITS - 2, chunk],
            recv_sem=relay_recv.at[chunk],
            device_id=next_wide,
            device_id_type=MESH,
        )

    def pass_on(chunk):
        rows = pl.ds(pl.multiple_of(chunk * CHUNK, CHUNK), CHUNK)
        return pltpu.make_async_remote_copy(
            src_ref=relay.at[rows],
            dst_ref=held.at[VISITS - 1, rows],
            send_sem=relay_send.at[chunk],
            recv_sem=recv_sem.at[VISITS - 2, chunk],
            device_id=next_run,
            device_id_type=MESH,
        )

    def send_guest(visit, slot):
        chunk = slot + GBASE
        rows = pl.ds(pl.multiple_of(chunk * CHUNK, CHUNK), CHUNK)
        return pltpu.make_async_remote_copy(
            src_ref=fresh.at[visit, rows],
            dst_ref=guest.at[visit],
            send_sem=send_sem.at[visit, chunk],
            recv_sem=guest_recv.at[visit],
            device_id=host_of(slot),
            device_id_type=MESH,
        )

    def guest_on(visit):
        chunk = guest_slot + GBASE
        rows = pl.ds(pl.multiple_of(chunk * CHUNK, CHUNK), CHUNK)
        return pltpu.make_async_remote_copy(
            src_ref=guest.at[visit],
            dst_ref=held.at[visit + 1, rows],
            send_sem=guest_send.at[visit],
            recv_sem=recv_sem.at[visit, chunk],
            device_id=guest_to,
            device_id_type=MESH,
        )

    def serve(visit):
        @pl.when(is_host)
        def _():
            send_guest(visit, 0).wait_recv()
            guest_on(visit).start()

    def dispatch(visit, chunk):
        if visit < VISITS - 2:
            apart = is_last & odd & (chunk >= GBASE) & (chunk < GBASE + GUESTS)

            @pl.when(apart)
            def _():
                send_guest(visit, jnp.clip(chunk - GBASE, 0, GUESTS - 1)).start()

            @pl.when(jnp.logical_not(apart))
            def _():
                send(visit, chunk).start()
        elif visit == VISITS - 2:
            @pl.when(is_last)
            def _():
                send_around(chunk).start()

            @pl.when(jnp.logical_not(is_last))
            def _():
                send(visit, chunk).start()

    def forward(chunk):
        @pl.when(is_first)
        def _():
            send_around(chunk).wait_recv()
            pass_on(chunk).start()

    def update(visit, chunk):
        rows = pl.ds(pl.multiple_of(chunk * CHUNK, CHUNK), CHUNK)
        old = held[visit, rows, :]
        low_frames = low[...]
        predicted = lax.dot_general(
            low_frames, old, (((1,), (1,)), ((), ())), preferred_element_type=jnp.float32
        )
        place = visit * (width // LANES) + chunk
        columns = pl.ds(pl.multiple_of(place * LANES, LANES), LANES)
        words = bits[:, pl.ds(pl.multiple_of(lax.rem(place, groups) * LANES, LANES), LANES)]
        flag = jnp.left_shift(jnp.int32(1), lax.div(place, groups))
        errors = jnp.where((words & flag) != 0, obs[:, columns].astype(jnp.float32) - predicted, 0.0)
        scaled = jnp.clip(errors, -1.0, 1.0).astype(jnp.bfloat16)
        total[...] += jnp.dot(scaled, old, preferred_element_type=jnp.float32)
        grad = lax.dot_general(
            scaled, low_frames, (((0,), (0,)), ((), ())), preferred_element_type=jnp.float32
        )
        wide_old = old.astype(jnp.float32)
        new = (wide_old + step_pixels * (grad - decay_weight * wide_old)).astype(jnp.bfloat16)
        if visit < VISITS - 1:
            fresh[visit, rows, :] = new
        else:
            pixels_out[rows, :] = new

    for visit in range(VISITS):
        low[...] = frames[...].astype(jnp.bfloat16)
        total[...] = jnp.zeros_like(total)
        load_obs(visit).wait()

        if visit == 0:
            update(0, 0)
            meet()
            dispatch(0, 0)
        elif visit == VISITS - 1:
            for chunk in range(min(AHEAD, RELAYED)):
                forward(chunk)

        @pl.loop(1 if visit == 0 else 0, chunks)
        def _(chunk, visit=visit):
            if visit == VISITS - 1 and AHEAD < RELAYED:
                @pl.when(chunk + AHEAD < RELAYED)
                def _():
                    forward(chunk + AHEAD)

            if visit:
                send(visit - 1, chunk).wait_recv()
            update(visit, chunk)
            dispatch(visit, chunk)

        if visit == 0:
            serve(0)
            serve(1)
        elif visit == 1:
            serve(2)

        current = frames[...]
        updated = current + step_frames * (total[...] - decay_weight * current)
        if visit < VISITS - 1:
            frames[...] = updated
        else:
            frames_out[...] = updated

    for visit in range(VISITS - 1):
        @pl.loop(0, chunks)
        def _(chunk, visit=visit):
            send(visit, chunk).wait_send()

    @pl.when(is_host)
    def _():
        for visit in range(VISITS - 2):
            guest_on(visit).wait_send()

    @pl.when(is_first)
    def _():
        for chunk in range(RELAYED):
            pass_on(chunk).wait_send()


def solution(mesh):
    n_blk, n_wide = mesh.shape["blk"], mesh.shape["wide"]

    def body(observed, mask_bits, frame_factors, pixel_factors):
        width, rank = pixel_factors.shape
        chunks = width // CHUNK
        return tuple(pl.pallas_call(
            functools.partial(kernel, n_blk, n_wide),
            out_shape=(
                pltpu.VMEM(frame_factors.shape, frame_factors.dtype),
                pltpu.VMEM(pixel_factors.shape, pixel_factors.dtype),
            ),
            in_specs=[pl.BlockSpec(memory_space=pltpu.HBM)] * 4,
            out_specs=(pl.BlockSpec(memory_space=pltpu.VMEM),) * 2,
            scratch_shapes=[
                pltpu.VMEM(observed.shape, observed.dtype),
                pltpu.VMEM(mask_bits.shape, mask_bits.dtype),
                pltpu.VMEM(frame_factors.shape, jnp.float32),
                pltpu.VMEM(frame_factors.shape, jnp.bfloat16),
                pltpu.VMEM(frame_factors.shape, jnp.float32),
                pltpu.VMEM((VISITS, width, rank), jnp.bfloat16),
                pltpu.VMEM((VISITS - 1, width, rank), jnp.bfloat16),
                pltpu.VMEM((max(RELAYED, 1) * CHUNK, rank), jnp.bfloat16),
                pltpu.SemaphoreType.DMA((3 + VISITS,)),
                pltpu.SemaphoreType.DMA((VISITS - 1, chunks)),
                pltpu.SemaphoreType.DMA((VISITS - 1, chunks)),
                pltpu.SemaphoreType.DMA((chunks,)),
                pltpu.SemaphoreType.DMA((chunks,)),
                pltpu.VMEM((VISITS - 2, CHUNK, rank), jnp.bfloat16),
                pltpu.SemaphoreType.DMA((VISITS - 2,)),
                pltpu.SemaphoreType.DMA((VISITS - 2,)),
            ],
            compiler_params=pltpu.CompilerParams(
                collective_id=0, has_side_effects=True, vmem_limit_bytes=20 << 20
            ),
        )(*(pltpu.with_memory_space_constraint(x, pltpu.HBM) for x in (observed, mask_bits, frame_factors, pixel_factors))))

    spec = P(("blk", "wide"), None)
    return jax.shard_map(
        body, mesh=mesh, in_specs=(spec,) * 4, out_specs=(spec, spec), check_vma=False
    )
```

```python
import functools

import jax
import jax.numpy as jnp
from jax import lax
from jax.experimental import pallas as pl
from jax.experimental.pallas import tpu as pltpu
from jax.sharding import PartitionSpec as P

VISITS = 5
LANES = 128
CHUNK = 128
RUN = 8
RELAYED = 5
AHEAD = 4
GBASE = 6
GUESTS = 2
MESH = pl.DeviceIdType.MESH

step_frames = 0.01
step_pixels = 0.02
decay_weight = 0.1


def kernel(
    n_blk, n_wide, obs_hbm, bits_hbm, frames_hbm, pixels_hbm, frames_out, pixels_out,
    obs, bits, frames, low, total, held, fresh, relay, load_sem, send_sem, recv_sem, relay_send, relay_recv,
    guest, guest_send, guest_recv,
):
    width = pixels_out.shape[0]
    chunks = width // CHUNK
    groups = bits.shape[1] // LANES
    i, j = lax.axis_index("blk"), lax.axis_index("wide")
    next_blk = (lax.rem(i + 1, n_blk), j)
    last_blk = (lax.rem(i + n_blk - 1, n_blk), j)
    place = lax.rem(j, RUN)
    is_first, is_last = place == 0, place == RUN - 1
    next_wide = (i, jnp.where(is_last, j - (RUN - 1), j + 1))
    last_wide = (i, jnp.where(is_first, j + (RUN - 1), j - 1))
    next_run = (i, lax.rem(j + RUN, n_wide))
    last_run = (i, lax.rem(j + n_wide - RUN, n_wide))
    right = (i, lax.rem(j + 1, n_wide))
    left = (i, lax.rem(j + n_wide - 1, n_wide))

    barrier = pltpu.get_barrier_semaphore()

    def greet(peer):
        pl.semaphore_signal(barrier, inc=1, device_id=peer, device_id_type=MESH)

    for peer in (last_blk, left):
        greet(peer)

    odd = lax.rem(i, 2) == 1
    even = jnp.logical_not(odd)
    is_host = even & (place < RUN - 1) & (place >= RUN - 1 - GUESTS)
    guest_slot = jnp.where(is_host, RUN - 2 - place, 0)
    guest_from = (lax.rem(i + 1, n_blk), jnp.where(is_host, j + guest_slot + 1, j))
    guest_to = (lax.rem(i + 2, n_blk), guest_from[1])

    def host_of(chunk):
        return (lax.rem(i + n_blk - 1, n_blk), jnp.where(is_last, j - 1 - chunk, j))

    @pl.when(is_host)
    def _():
        greet(guest_from)

    @pl.when(is_last & even)
    def _():
        for chunk in range(GUESTS):
            greet((lax.rem(i + n_blk - 2, n_blk), host_of(chunk)[1]))

    @pl.when(is_first)
    def _():
        greet(last_wide)
        greet(last_run)

    def meet():
        extra = jnp.where(is_host | is_first, 1, jnp.where(is_last, 1 + jnp.where(odd, GUESTS, 0), 0))
        pl.semaphore_wait(barrier, 2 + extra)

    def load(source, target, index):
        return pltpu.make_async_copy(source, target, load_sem.at[index])

    def load_obs(visit):
        start = CHUNK if visit == 0 else visit * width
        columns = pl.ds(start, (visit + 1) * width - start)
        return load(obs_hbm.at[:, columns], obs.at[:, columns], 3 + visit)

    head, tail, lane_tail = pl.ds(0, CHUNK), pl.ds(CHUNK, width - CHUNK), pl.ds(LANES, bits.shape[1] - LANES)
    first = [
        load(frames_hbm, frames, 0),
        load(pixels_hbm.at[head], held.at[0, head], 1),
        load(bits_hbm.at[:, pl.ds(0, LANES)], bits.at[:, pl.ds(0, LANES)], 2),
        load(obs_hbm.at[:, head], obs.at[:, head], 3 + VISITS),
    ]
    second = [
        load(pixels_hbm.at[tail], held.at[0, tail], 4 + VISITS),
        load(bits_hbm.at[:, lane_tail], bits.at[:, lane_tail], 5 + VISITS),
    ]
    for copy in first + second:
        copy.start()
    for visit in range(VISITS):
        load_obs(visit).start()
    for copy in first:
        copy.wait()

    def send(visit, chunk):
        rows = pl.ds(pl.multiple_of(chunk * CHUNK, CHUNK), CHUNK)
        return pltpu.make_async_remote_copy(
            src_ref=fresh.at[visit, rows],
            dst_ref=held.at[visit + 1, rows],
            send_sem=send_sem.at[visit, chunk],
            recv_sem=recv_sem.at[visit, chunk],
            device_id=next_blk if visit < VISITS - 2 else right,
            device_id_type=MESH,
        )

    def send_around(chunk):
        chunk = jnp.minimum(chunk, RELAYED - 1)
        rows = pl.ds(pl.multiple_of(chunk * CHUNK, CHUNK), CHUNK)
        return pltpu.make_async_remote_copy(
            src_ref=fresh.at[VISITS - 2, rows],
            dst_ref=relay.at[rows],
            send_sem=send_sem.at[VISITS - 2, chunk],
            recv_sem=relay_recv.at[chunk],
            device_id=next_wide,
            device_id_type=MESH,
        )

    def pass_on(chunk):
        rows = pl.ds(pl.multiple_of(chunk * CHUNK, CHUNK), CHUNK)
        return pltpu.make_async_remote_copy(
            src_ref=relay.at[rows],
            dst_ref=held.at[VISITS - 1, rows],
            send_sem=relay_send.at[chunk],
            recv_sem=recv_sem.at[VISITS - 2, chunk],
            device_id=next_run,
            device_id_type=MESH,
        )

    def send_guest(visit, slot):
        chunk = slot + GBASE
        rows = pl.ds(pl.multiple_of(chunk * CHUNK, CHUNK), CHUNK)
        return pltpu.make_async_remote_copy(
            src_ref=fresh.at[visit, rows],
            dst_ref=guest.at[visit],
            send_sem=send_sem.at[visit, chunk],
            recv_sem=guest_recv.at[visit],
            device_id=host_of(slot),
            device_id_type=MESH,
        )

    def guest_on(visit):
        chunk = guest_slot + GBASE
        rows = pl.ds(pl.multiple_of(chunk * CHUNK, CHUNK), CHUNK)
        return pltpu.make_async_remote_copy(
            src_ref=guest.at[visit],
            dst_ref=held.at[visit + 1, rows],
            send_sem=guest_send.at[visit],
            recv_sem=recv_sem.at[visit, chunk],
            device_id=guest_to,
            device_id_type=MESH,
        )

    def serve(visit):
        @pl.when(is_host)
        def _():
            send_guest(visit, 0).wait_recv()
            guest_on(visit).start()

    def dispatch(visit, chunk):
        if visit < VISITS - 2:
            apart = is_last & odd & (chunk >= GBASE) & (chunk < GBASE + GUESTS)

            @pl.when(apart)
            def _():
                send_guest(visit, jnp.clip(chunk - GBASE, 0, GUESTS - 1)).start()

            @pl.when(jnp.logical_not(apart))
            def _():
                send(visit, chunk).start()
        elif visit == VISITS - 2:
            around = is_last & (chunk < RELAYED)

            @pl.when(around)
            def _():
                send_around(chunk).start()

            @pl.when(jnp.logical_not(around))
            def _():
                send(visit, chunk).start()

    def forward(chunk):
        @pl.when(is_first)
        def _():
            send_around(chunk).wait_recv()
            pass_on(chunk).start()

    def update(visit, chunk):
        rows = pl.ds(pl.multiple_of(chunk * CHUNK, CHUNK), CHUNK)
        old = held[visit, rows, :]
        low_frames = low[...]
        predicted = lax.dot_general(
            low_frames, old, (((1,), (1,)), ((), ())), preferred_element_type=jnp.float32
        )
        place = visit * (width // LANES) + chunk
        columns = pl.ds(pl.multiple_of(place * LANES, LANES), LANES)
        words = bits[:, pl.ds(pl.multiple_of(lax.rem(place, groups) * LANES, LANES), LANES)]
        flag = jnp.left_shift(jnp.int32(1), lax.div(place, groups))
        errors = jnp.where((words & flag) != 0, obs[:, columns].astype(jnp.float32) - predicted, 0.0)
        scaled = jnp.clip(errors, -1.0, 1.0).astype(jnp.bfloat16)
        total[...] += jnp.dot(scaled, old, preferred_element_type=jnp.float32)
        grad = lax.dot_general(
            scaled, low_frames, (((0,), (0,)), ((), ())), preferred_element_type=jnp.float32
        )
        wide_old = old.astype(jnp.float32)
        new = (wide_old + step_pixels * (grad - decay_weight * wide_old)).astype(jnp.bfloat16)
        if visit < VISITS - 1:
            fresh[visit, rows, :] = new
        else:
            pixels_out[rows, :] = new

    for visit in range(VISITS):
        low[...] = frames[...].astype(jnp.bfloat16)
        total[...] = jnp.zeros_like(total)

        if visit == 0:
            update(0, 0)
            meet()
            dispatch(0, 0)
            for copy in second:
                copy.wait()
        load_obs(visit).wait()

        if visit == VISITS - 1:
            for chunk in range(min(AHEAD, RELAYED)):
                forward(chunk)

        @pl.loop(1 if visit == 0 else 0, chunks)
        def _(chunk, visit=visit):
            if visit == VISITS - 1 and AHEAD < RELAYED:
                @pl.when(chunk + AHEAD < RELAYED)
                def _():
                    forward(chunk + AHEAD)

            if visit:
                send(visit - 1, chunk).wait_recv()
            update(visit, chunk)
            dispatch(visit, chunk)

        if visit == 0:
            serve(0)
            serve(1)
        elif visit == 1:
            serve(2)

        current = frames[...]
        updated = current + step_frames * (total[...] - decay_weight * current)
        if visit < VISITS - 1:
            frames[...] = updated
        else:
            frames_out[...] = updated

    for visit in range(VISITS - 1):
        @pl.loop(0, chunks)
        def _(chunk, visit=visit):
            send(visit, chunk).wait_send()

    @pl.when(is_host)
    def _():
        for visit in range(VISITS - 2):
            guest_on(visit).wait_send()

    @pl.when(is_first)
    def _():
        for chunk in range(RELAYED):
            pass_on(chunk).wait_send()


def store_kernel(frames, pixels, frames_out, pixels_out, sem):
    copies = [
        pltpu.make_async_copy(frames, frames_out, sem.at[0]),
        pltpu.make_async_copy(pixels, pixels_out, sem.at[1]),
    ]
    for copy in copies:
        copy.start()
    for copy in copies:
        copy.wait()


def store(frames, pixels):
    return pl.pallas_call(
        store_kernel,
        out_shape=(
            jax.ShapeDtypeStruct(frames.shape, frames.dtype),
            jax.ShapeDtypeStruct(pixels.shape, pixels.dtype),
        ),
        in_specs=[pl.BlockSpec(memory_space=pltpu.VMEM)] * 2,
        out_specs=(pl.BlockSpec(memory_space=pl.ANY),) * 2,
        scratch_shapes=[pltpu.SemaphoreType.DMA((2,))],
        compiler_params=pltpu.CompilerParams(vmem_limit_bytes=8 << 20),
    )(frames, pixels)


def solution(mesh):
    n_blk, n_wide = mesh.shape["blk"], mesh.shape["wide"]

    def body(observed, mask_bits, frame_factors, pixel_factors):
        width, rank = pixel_factors.shape
        chunks = width // CHUNK
        return store(*pl.pallas_call(
            functools.partial(kernel, n_blk, n_wide),
            out_shape=(
                pltpu.VMEM(frame_factors.shape, frame_factors.dtype),
                pltpu.VMEM(pixel_factors.shape, pixel_factors.dtype),
            ),
            in_specs=[pl.BlockSpec(memory_space=pltpu.HBM)] * 4,
            out_specs=(pl.BlockSpec(memory_space=pltpu.VMEM),) * 2,
            scratch_shapes=[
                pltpu.VMEM(observed.shape, observed.dtype),
                pltpu.VMEM(mask_bits.shape, mask_bits.dtype),
                pltpu.VMEM(frame_factors.shape, jnp.float32),
                pltpu.VMEM(frame_factors.shape, jnp.bfloat16),
                pltpu.VMEM(frame_factors.shape, jnp.float32),
                pltpu.VMEM((VISITS, width, rank), jnp.bfloat16),
                pltpu.VMEM((VISITS - 1, width, rank), jnp.bfloat16),
                pltpu.VMEM((max(RELAYED, 1) * CHUNK, rank), jnp.bfloat16),
                pltpu.SemaphoreType.DMA((6 + VISITS,)),
                pltpu.SemaphoreType.DMA((VISITS - 1, chunks)),
                pltpu.SemaphoreType.DMA((VISITS - 1, chunks)),
                pltpu.SemaphoreType.DMA((chunks,)),
                pltpu.SemaphoreType.DMA((chunks,)),
                pltpu.VMEM((VISITS - 2, CHUNK, rank), jnp.bfloat16),
                pltpu.SemaphoreType.DMA((VISITS - 2,)),
                pltpu.SemaphoreType.DMA((VISITS - 2,)),
            ],
            compiler_params=pltpu.CompilerParams(
                collective_id=0, has_side_effects=True, vmem_limit_bytes=20 << 20
            ),
        )(*(pltpu.with_memory_space_constraint(x, pltpu.HBM) for x in (observed, mask_bits, frame_factors, pixel_factors))))

    spec = P(("blk", "wide"), None)
    return jax.shard_map(
        body, mesh=mesh, in_specs=(spec,) * 4, out_specs=(spec, spec), check_vma=False
    )
```

```python
import functools

import jax
import jax.numpy as jnp
from jax import lax
from jax.experimental import pallas as pl
from jax.experimental.pallas import tpu as pltpu
from jax.sharding import PartitionSpec as P

VISITS = 5
LANES = 128
CHUNK = 128
RUN = 8
RELAYED = 3
AHEAD = 3
GBASE = 5
GUESTS = 3
MESH = pl.DeviceIdType.MESH

step_frames = 0.01
step_pixels = 0.02
decay_weight = 0.1


def kernel(
    n_blk, n_wide, obs_hbm, bits_hbm, frames_hbm, pixels_hbm, frames_out, pixels_out,
    obs, bits, frames, low, total, held, fresh, relay, load_sem, send_sem, recv_sem, relay_send, relay_recv,
    guest, guest_send, guest_recv,
):
    width = pixels_out.shape[0]
    chunks = width // CHUNK
    groups = bits.shape[1] // LANES
    i, j = lax.axis_index("blk"), lax.axis_index("wide")
    next_blk = (lax.rem(i + 1, n_blk), j)
    last_blk = (lax.rem(i + n_blk - 1, n_blk), j)
    place = lax.rem(j, RUN)
    is_first, is_last = place == 0, place == RUN - 1
    next_wide = (i, jnp.where(is_last, j - (RUN - 1), j + 1))
    last_wide = (i, jnp.where(is_first, j + (RUN - 1), j - 1))
    next_run = (i, lax.rem(j + RUN, n_wide))
    last_run = (i, lax.rem(j + n_wide - RUN, n_wide))
    right = (i, lax.rem(j + 1, n_wide))
    left = (i, lax.rem(j + n_wide - 1, n_wide))

    barrier = pltpu.get_barrier_semaphore()

    def greet(peer):
        pl.semaphore_signal(barrier, inc=1, device_id=peer, device_id_type=MESH)

    for peer in (last_blk, left):
        greet(peer)

    odd = lax.rem(i, 2) == 1
    even = jnp.logical_not(odd)
    is_host = even & (place < RUN - 1) & (place >= RUN - 1 - GUESTS)
    guest_slot = jnp.where(is_host, RUN - 2 - place, 0)
    guest_from = (lax.rem(i + 1, n_blk), jnp.where(is_host, j + guest_slot + 1, j))
    guest_to = (lax.rem(i + 2, n_blk), guest_from[1])

    def host_of(chunk):
        return (lax.rem(i + n_blk - 1, n_blk), jnp.where(is_last, j - 1 - chunk, j))

    @pl.when(is_host)
    def _():
        greet(guest_from)

    @pl.when(is_last & even)
    def _():
        for chunk in range(GUESTS):
            greet((lax.rem(i + n_blk - 2, n_blk), host_of(chunk)[1]))

    @pl.when(is_first)
    def _():
        greet(last_wide)
        greet(last_run)

    def meet():
        extra = jnp.where(is_host | is_first, 1, jnp.where(is_last, 1 + jnp.where(odd, GUESTS, 0), 0))
        pl.semaphore_wait(barrier, 2 + extra)

    def load(source, target, index):
        return pltpu.make_async_copy(source, target, load_sem.at[index])

    def load_obs(visit):
        start = CHUNK if visit == 0 else visit * width
        columns = pl.ds(start, (visit + 1) * width - start)
        return load(obs_hbm.at[:, columns], obs.at[:, columns], 3 + visit)

    head, tail, lane_tail = pl.ds(0, CHUNK), pl.ds(CHUNK, width - CHUNK), pl.ds(LANES, bits.shape[1] - LANES)
    first = [
        load(frames_hbm, frames, 0),
        load(pixels_hbm.at[head], held.at[0, head], 1),
        load(bits_hbm.at[:, pl.ds(0, LANES)], bits.at[:, pl.ds(0, LANES)], 2),
        load(obs_hbm.at[:, head], obs.at[:, head], 3 + VISITS),
    ]
    second = [
        load(pixels_hbm.at[tail], held.at[0, tail], 4 + VISITS),
        load(bits_hbm.at[:, lane_tail], bits.at[:, lane_tail], 5 + VISITS),
    ]
    for copy in first + second:
        copy.start()
    for visit in range(VISITS):
        load_obs(visit).start()
    for copy in first:
        copy.wait()

    def send(visit, chunk):
        rows = pl.ds(pl.multiple_of(chunk * CHUNK, CHUNK), CHUNK)
        return pltpu.make_async_remote_copy(
            src_ref=fresh.at[visit, rows],
            dst_ref=held.at[visit + 1, rows],
            send_sem=send_sem.at[visit, chunk],
            recv_sem=recv_sem.at[visit, chunk],
            device_id=next_blk if visit < VISITS - 2 else right,
            device_id_type=MESH,
        )

    def send_around(chunk):
        chunk = jnp.minimum(chunk, RELAYED - 1)
        rows = pl.ds(pl.multiple_of(chunk * CHUNK, CHUNK), CHUNK)
        return pltpu.make_async_remote_copy(
            src_ref=fresh.at[VISITS - 2, rows],
            dst_ref=relay.at[rows],
            send_sem=send_sem.at[VISITS - 2, chunk],
            recv_sem=relay_recv.at[chunk],
            device_id=next_wide,
            device_id_type=MESH,
        )

    def pass_on(chunk):
        rows = pl.ds(pl.multiple_of(chunk * CHUNK, CHUNK), CHUNK)
        return pltpu.make_async_remote_copy(
            src_ref=relay.at[rows],
            dst_ref=held.at[VISITS - 1, rows],
            send_sem=relay_send.at[chunk],
            recv_sem=recv_sem.at[VISITS - 2, chunk],
            device_id=next_run,
            device_id_type=MESH,
        )

    def send_guest(visit, slot):
        chunk = slot + GBASE
        rows = pl.ds(pl.multiple_of(chunk * CHUNK, CHUNK), CHUNK)
        return pltpu.make_async_remote_copy(
            src_ref=fresh.at[visit, rows],
            dst_ref=guest.at[visit],
            send_sem=send_sem.at[visit, chunk],
            recv_sem=guest_recv.at[visit],
            device_id=host_of(slot),
            device_id_type=MESH,
        )

    def guest_on(visit):
        chunk = guest_slot + GBASE
        rows = pl.ds(pl.multiple_of(chunk * CHUNK, CHUNK), CHUNK)
        return pltpu.make_async_remote_copy(
            src_ref=guest.at[visit],
            dst_ref=held.at[visit + 1, rows],
            send_sem=guest_send.at[visit],
            recv_sem=recv_sem.at[visit, chunk],
            device_id=guest_to,
            device_id_type=MESH,
        )

    def serve(visit):
        @pl.when(is_host)
        def _():
            send_guest(visit, 0).wait_recv()
            guest_on(visit).start()

    def dispatch(visit, chunk):
        if visit < VISITS - 2:
            apart = is_last & odd & (chunk >= GBASE) & (chunk < GBASE + GUESTS)

            @pl.when(apart)
            def _():
                send_guest(visit, jnp.clip(chunk - GBASE, 0, GUESTS - 1)).start()

            @pl.when(jnp.logical_not(apart))
            def _():
                send(visit, chunk).start()
        elif visit == VISITS - 2:
            around = is_last & (chunk < RELAYED)

            @pl.when(around)
            def _():
                send_around(chunk).start()

            @pl.when(jnp.logical_not(around))
            def _():
                send(visit, chunk).start()

    def forward(chunk):
        @pl.when(is_first)
        def _():
            send_around(chunk).wait_recv()
            pass_on(chunk).start()

    def update(visit, chunk):
        rows = pl.ds(pl.multiple_of(chunk * CHUNK, CHUNK), CHUNK)
        old = held[visit, rows, :]
        low_frames = low[...]
        predicted = lax.dot_general(
            low_frames, old, (((1,), (1,)), ((), ())), preferred_element_type=jnp.float32
        )
        place = visit * (width // LANES) + chunk
        columns = pl.ds(pl.multiple_of(place * LANES, LANES), LANES)
        words = bits[:, pl.ds(pl.multiple_of(lax.rem(place, groups) * LANES, LANES), LANES)]
        flag = jnp.left_shift(jnp.int32(1), lax.div(place, groups))
        errors = jnp.where((words & flag) != 0, obs[:, columns].astype(jnp.float32) - predicted, 0.0)
        scaled = jnp.clip(errors, -1.0, 1.0).astype(jnp.bfloat16)
        total[...] += jnp.dot(scaled, old, preferred_element_type=jnp.float32)
        grad = lax.dot_general(
            scaled, low_frames, (((0,), (0,)), ((), ())), preferred_element_type=jnp.float32
        )
        wide_old = old.astype(jnp.float32)
        new = (wide_old + step_pixels * (grad - decay_weight * wide_old)).astype(jnp.bfloat16)
        if visit < VISITS - 1:
            fresh[visit, rows, :] = new
        else:
            pixels_out[rows, :] = new

    for visit in range(VISITS):
        low[...] = frames[...].astype(jnp.bfloat16)
        total[...] = jnp.zeros_like(total)

        if visit == 0:
            update(0, 0)
            meet()
            dispatch(0, 0)
            for copy in second:
                copy.wait()
        load_obs(visit).wait()

        if visit == VISITS - 1:
            for chunk in range(min(AHEAD, RELAYED)):
                forward(chunk)

        @pl.loop(1 if visit == 0 else 0, chunks)
        def _(chunk, visit=visit):
            if visit == VISITS - 1 and AHEAD < RELAYED:
                @pl.when(chunk + AHEAD < RELAYED)
                def _():
                    forward(chunk + AHEAD)

            if visit:
                send(visit - 1, chunk).wait_recv()
            update(visit, chunk)
            dispatch(visit, chunk)

        if visit == 0:
            serve(0)
            serve(1)
        elif visit == 1:
            serve(2)

        current = frames[...]
        updated = current + step_frames * (total[...] - decay_weight * current)
        if visit < VISITS - 1:
            frames[...] = updated
        else:
            frames_out[...] = updated

    for visit in range(VISITS - 1):
        @pl.loop(0, chunks)
        def _(chunk, visit=visit):
            send(visit, chunk).wait_send()

    @pl.when(is_host)
    def _():
        for visit in range(VISITS - 2):
            guest_on(visit).wait_send()

    @pl.when(is_first)
    def _():
        for chunk in range(RELAYED):
            pass_on(chunk).wait_send()


def store_kernel(frames, pixels, frames_out, pixels_out, sem):
    copies = [
        pltpu.make_async_copy(frames, frames_out, sem.at[0]),
        pltpu.make_async_copy(pixels, pixels_out, sem.at[1]),
    ]
    for copy in copies:
        copy.start()
    for copy in copies:
        copy.wait()


def store(frames, pixels):
    return pl.pallas_call(
        store_kernel,
        out_shape=(
            jax.ShapeDtypeStruct(frames.shape, frames.dtype),
            jax.ShapeDtypeStruct(pixels.shape, pixels.dtype),
        ),
        in_specs=[pl.BlockSpec(memory_space=pltpu.VMEM)] * 2,
        out_specs=(pl.BlockSpec(memory_space=pl.ANY),) * 2,
        scratch_shapes=[pltpu.SemaphoreType.DMA((2,))],
        compiler_params=pltpu.CompilerParams(vmem_limit_bytes=8 << 20),
    )(frames, pixels)


def solution(mesh):
    n_blk, n_wide = mesh.shape["blk"], mesh.shape["wide"]

    def body(observed, mask_bits, frame_factors, pixel_factors):
        width, rank = pixel_factors.shape
        chunks = width // CHUNK
        return store(*pl.pallas_call(
            functools.partial(kernel, n_blk, n_wide),
            out_shape=(
                pltpu.VMEM(frame_factors.shape, frame_factors.dtype),
                pltpu.VMEM(pixel_factors.shape, pixel_factors.dtype),
            ),
            in_specs=[pl.BlockSpec(memory_space=pltpu.HBM)] * 4,
            out_specs=(pl.BlockSpec(memory_space=pltpu.VMEM),) * 2,
            scratch_shapes=[
                pltpu.VMEM(observed.shape, observed.dtype),
                pltpu.VMEM(mask_bits.shape, mask_bits.dtype),
                pltpu.VMEM(frame_factors.shape, jnp.float32),
                pltpu.VMEM(frame_factors.shape, jnp.bfloat16),
                pltpu.VMEM(frame_factors.shape, jnp.float32),
                pltpu.VMEM((VISITS, width, rank), jnp.bfloat16),
                pltpu.VMEM((VISITS - 1, width, rank), jnp.bfloat16),
                pltpu.VMEM((max(RELAYED, 1) * CHUNK, rank), jnp.bfloat16),
                pltpu.SemaphoreType.DMA((6 + VISITS,)),
                pltpu.SemaphoreType.DMA((VISITS - 1, chunks)),
                pltpu.SemaphoreType.DMA((VISITS - 1, chunks)),
                pltpu.SemaphoreType.DMA((chunks,)),
                pltpu.SemaphoreType.DMA((chunks,)),
                pltpu.VMEM((VISITS - 2, CHUNK, rank), jnp.bfloat16),
                pltpu.SemaphoreType.DMA((VISITS - 2,)),
                pltpu.SemaphoreType.DMA((VISITS - 2,)),
            ],
            compiler_params=pltpu.CompilerParams(
                collective_id=0, has_side_effects=True, vmem_limit_bytes=20 << 20
            ),
        )(*(pltpu.with_memory_space_constraint(x, pltpu.HBM) for x in (observed, mask_bits, frame_factors, pixel_factors))))

    spec = P(("blk", "wide"), None)
    return jax.shard_map(
        body, mesh=mesh, in_specs=(spec,) * 4, out_specs=(spec, spec), check_vma=False
    )
```
